128 devices in a mesh: chain: 2 (over core), energy: 64 (over z, y, x).
Axes of the slice: x: 4, y: 4, z: 4, core: 2. Of those that a mesh axis runs over, the one named last changes fastest.
Arguments:
- retarded: float32 [64, 4, 2, 256, 256], P('energy', 'chain'), may hold values from -0.625 to 0.625
- lesser_sigma: float32 [64, 4, 2, 256, 256], P('energy', 'chain'), may hold values from -6 to 6
- coupling: float32 [4, 2, 256, 256], P('chain'), may hold values from -1 to 1
- coupling_pattern: int32 [4, 4, 4], P('chain'), may hold values from 0 to 1, as said below
- kept_blocks: int32 [4], replicated, may hold values from 0 to 15, as said below
- lead_lesser: float32 [64, 2, 256, 256], P('energy'), may hold values from -8 to 8
Outputs:
- polarization: float32 [16, 2, 65536], P(None, None, ('chain', 'energy'))
The draws below stay inside these ranges and needn't reach their ends.
Inputs may be any that keep to these rules, and one draw needn't show every extreme that they name: `coupling_pattern`: 0/1 entries; each cell's coupling has exactly 4 ones. `kept_blocks`: distinct block numbers.
All inputs are finite; a program needn't handle non-finite values.
Results may differ from the reference program's by a relative error of at most 0.0001.
Values sent between devices are 32-bit elements; how exact they have to be, the bound alone decides.
A program may use at most 832 MiB of HBM per device.

```python
import jax
import jax.numpy as jnp
from jax import lax

M = 256
BLOCK = 64
NBLK = 4
KEEP = 4
B_NNZ = 4
LAGS = 16
ENERGIES = 64
NCELLS = 4
ELEMS = 65536


def draw_coupling_pattern(key, part):
    subkeys = jax.random.split(jax.random.fold_in(key, 11), NCELLS)
    orders = jax.vmap(lambda one_key: jax.random.permutation(one_key, NBLK * NBLK))(subkeys)
    return (orders < B_NNZ).astype(jnp.int32).reshape(NCELLS, NBLK, NBLK)


def draw_kept_blocks(key, part):
    middle = jax.random.permutation(jax.random.fold_in(key, 12), NBLK * NBLK - 2) + 1
    first = jnp.zeros((1,), jnp.int32)
    last = jnp.full((1,), NBLK * NBLK - 1, jnp.int32)
    chosen = jnp.concatenate([first, middle[:KEEP - 2].astype(jnp.int32), last])
    return jax.random.permutation(jax.random.fold_in(key, 13), chosen).astype(jnp.int32)


def level_of(rng, dims, shards, smallest, largest):
    def one(dim, blocks):
        draws = jax.random.uniform(jax.random.fold_in(jax.random.fold_in(rng, 6), dim), (blocks,), jnp.float32, smallest / len(shards), largest / len(shards))
        return jnp.repeat(jnp.exp(draws), dims[dim] // blocks).reshape((-1,) + (1,) * (len(dims) - dim - 1))

    gain = one(*shards[0])
    for cut in shards[1:]:
        gain = gain * one(*cut)
    return gain


def gaussian(key, dims, width, limit, shards=(), kind=jnp.bfloat16):
    result = jax.random.normal(key, dims, jnp.float32) * width
    if len(shards) > 0:
        result = level_of(key, dims, shards, -0.22, 0.18) * result
    return jnp.clip(result, min=-limit, max=limit).astype(kind)


def setup_inputs(seed: int = 0) -> dict:
    seeds = jax.random.split(jax.random.key(seed), 7)
    return {
        "retarded": gaussian(seeds[0], (ENERGIES, NCELLS, 2, M, M), ((0.5 / M) ** 0.5), 0.625, ((0, 64), (1, 2)), jnp.float32),
        "lesser_sigma": gaussian(seeds[1], (ENERGIES, NCELLS, 2, M, M), 1.0, 6.0, ((0, 64), (1, 2)), jnp.float32),
        "coupling": gaussian(seeds[2], (NCELLS, 2, M, M), ((0.35 * NBLK * NBLK / (B_NNZ * M)) ** 0.5), 1.0, ((0, 2),), jnp.float32),
        "coupling_pattern": draw_coupling_pattern(jax.random.fold_in(seeds[6], 71), 0),
        "kept_blocks": draw_kept_blocks(jax.random.fold_in(seeds[6], 71), 0),
        "lead_lesser": gaussian(seeds[5], (ENERGIES, 2, M, M), 1.4, 8.0, ((0, 64),), jnp.float32),
    }


def matmul_high(left, right):
    return jnp.matmul(left, right, precision=lax.Precision.HIGHEST)


def complex_product(left, right):
    left_re, left_im = left[..., 0, :, :], left[..., 1, :, :]
    right_re, right_im = right[..., 0, :, :], right[..., 1, :, :]
    real_part = matmul_high(left_re, right_re) - matmul_high(left_im, right_im)
    imag_part = matmul_high(left_re, right_im) + matmul_high(left_im, right_re)
    return jnp.stack([real_part, imag_part], axis=-3)


def product_adjoint(left, right):
    left_re, left_im = left[..., 0, :, :], left[..., 1, :, :]
    right_tr = jnp.swapaxes(right[..., 0, :, :], -1, -2)
    right_ti = jnp.swapaxes(right[..., 1, :, :], -1, -2)
    real_part = matmul_high(left_re, right_tr) + matmul_high(left_im, right_ti)
    imag_part = matmul_high(left_im, right_tr) - matmul_high(left_re, right_ti)
    return jnp.stack([real_part, imag_part], axis=-3)


def expand_pattern(pattern):
    return jnp.repeat(jnp.repeat(pattern.astype(jnp.float32), BLOCK, axis=-2), BLOCK, axis=-1)


def pick_blocks(matrix, kept_blocks):
    lead_shape = matrix.shape[:-2]
    tiles = matrix.reshape(lead_shape + (NBLK, BLOCK, NBLK, BLOCK))
    tiles = jnp.swapaxes(tiles, -3, -2)
    tiles = tiles.reshape(lead_shape + (NBLK * NBLK, BLOCK * BLOCK))
    return jnp.take(tiles, kept_blocks, axis=-2)


def reference(retarded, lesser_sigma, coupling, coupling_pattern, kept_blocks, lead_lesser):
    coupling_full = coupling * expand_pattern(coupling_pattern)[:, None]

    def one_energy(operands):
        green_e, sigma_e, entry_block = operands

        def advance(state_in, inputs):
            green, sigma, bridge = inputs
            joined = complex_product(green, bridge)
            fresh = product_adjoint(complex_product(green, sigma), green)
            state_out = fresh + product_adjoint(complex_product(joined, state_in), joined)
            return state_out, pick_blocks(state_out, kept_blocks)

        _, retained = lax.scan(advance, entry_block, (green_e, sigma_e, coupling_full))
        return retained

    retained = lax.map(one_energy, (retarded, lesser_sigma, lead_lesser))
    retained = jnp.transpose(retained, (0, 2, 1, 3, 4)).reshape(ENERGIES, 2, ELEMS)
    results = []
    for lag_index in range(LAGS):
        shifted = retained[lag_index:]
        earlier = retained[:ENERGIES - lag_index]
        real_part = jnp.sum(shifted[:, 0] * earlier[:, 0] + shifted[:, 1] * earlier[:, 1], axis=0)
        imag_part = jnp.sum(shifted[:, 1] * earlier[:, 0] - shifted[:, 0] * earlier[:, 1], axis=0)
        results.append(jnp.stack([real_part, imag_part], axis=0))
    return jnp.stack(results, axis=0) / jnp.float32(ENERGIES)
```

```python
import functools

import jax
import jax.numpy as jnp
from jax import lax
from jax.experimental import pallas as pl
from jax.experimental.pallas import tpu as pltpu
from jax.sharding import PartitionSpec as P

M = 256
BLOCK = 64
NBLK = 4
KEEP = 4
LAGS = 16
ENERGIES = 64
SIDE = 4
MESH = pl.DeviceIdType.MESH
ADJ = (((1,), (1,)), ((), ()))
PLAIN = (((1,), (0,)), ((), ()))


def split(x):
    high = x.astype(jnp.bfloat16)
    return high, (x - high.astype(jnp.float32)).astype(jnp.bfloat16)


def dot3(left_h, left_l, right, dims):
    right_h, right_l = split(right)
    return lax.dot_general(
        jnp.concatenate([left_h, left_h, left_l], 1),
        jnp.concatenate([right_h, right_l, right_h], 1 if dims is ADJ else 0),
        dims,
        preferred_element_type=jnp.float32,
    )


class Left:
    def __init__(self, high, low):
        self.high, self.low = high, low

    def fill(self, re, im):
        for i, part in enumerate((re, im, re + im)):
            self.high[i], self.low[i] = split(part)

    def three(self, a, b, c, dims):
        return [dot3(self.high[i], self.low[i], x, dims) for i, x in enumerate((a, b, c))]

    def adjoint(self, re, im):
        p, q, s = self.three(re, im, re - im, ADJ)
        return p + q, s - p + q

    def plain(self, re, im):
        p, q, s = self.three(re, im, re + im, PLAIN)
        return p - q, s - p - q


def choose(which, blocks):
    out = blocks[-1]
    for i in range(len(blocks) - 2, -1, -1):
        out = jnp.where(which == i, blocks[i], out)
    return out


def row_blocks(part):
    return [part[i * BLOCK : (i + 1) * BLOCK] for i in range(NBLK)]


def kept_left(rows_ref, re, im, kept_rows):
    for k in range(KEEP):
        for i, part in enumerate((re, im)):
            high, low = split(choose(kept_rows[k], row_blocks(part)))
            rows_ref[k, :BLOCK, i * M : (i + 1) * M] = high
            rows_ref[k, BLOCK:, i * M : (i + 1) * M] = low


def kept_tiles(rows_ref, re, im, kept_cols):
    out = []
    for k in range(KEEP):
        re_h, re_l = split(choose(kept_cols[k], row_blocks(re)))
        im_h, im_l = split(choose(kept_cols[k], row_blocks(im)))
        stack = []
        for x, y in ((re_h, im_h), (re_l, im_l)):
            stack += [jnp.concatenate([x, y], 1), jnp.concatenate([-y, x], 1)]
        o = lax.dot_general(rows_ref[k], jnp.concatenate(stack, 0), ADJ, preferred_element_type=jnp.float32)
        o = o[:BLOCK] + o[BLOCK:]
        out.append(o[:, :128] + o[:, 128:])
    return out


def kernel(
    pattern_ref, kept_ref, g_hbm, s_hbm, b_hbm, lead_hbm, out_ref,
    g_in, s_in, b_in, lead_in, left_h, left_l, rows, right, passed, entered, send, recv, sums,
    in_sem, pass_sem, send_sem, recv_sem,
):
    chain, me = lax.axis_index("chain"), lax.axis_index("energy")
    my_y, my_x = lax.rem(lax.div(me, SIDE), SIDE), lax.rem(me, SIDE)

    def load(i, source, target):
        return pltpu.make_async_copy(source, target, in_sem.at[i])

    loads = {}
    for cell in range(2):
        loads["b", cell] = load(cell, b_hbm.at[cell], b_in.at[cell])
        loads["s", cell] = load(2 + cell, s_hbm.at[0, cell], s_in.at[cell])
        loads["g", cell] = load(4 + cell, g_hbm.at[0, cell], g_in.at[cell])
    loads["lead"] = load(6, lead_hbm.at[0], lead_in)
    for name in (("b", 0), "lead", ("s", 0), ("g", 0), ("b", 1), ("s", 1), ("g", 1)):
        loads[name].start()

    barrier = pltpu.get_barrier_semaphore()

    @pl.loop(1, ENERGIES)
    def _(step):
        pl.semaphore_signal(
            barrier, inc=1, device_id={"energy": lax.rem(me + step, ENERGIES)}, device_id_type=MESH
        )

    pl.semaphore_signal(barrier, inc=1, device_id={"chain": 1 - chain}, device_id_type=MESH)

    recv[pl.ds(ENERGIES, LAGS)] = jnp.zeros((LAGS, 8, 128), jnp.float32)
    lefts = [Left(left_h.at[i], left_l.at[i]) for i in range(5)]
    lane = lax.broadcasted_iota(jnp.int32, (BLOCK, 128), 1) < BLOCK

    def masked_coupling(cell):
        parts = []
        for part in range(2):
            rows = []
            for r in range(NBLK):
                strip = b_in[cell, part, r * BLOCK : (r + 1) * BLOCK, :]
                halves = []
                for t in range(NBLK // 2):
                    pair = [pattern_ref[cell, r, 2 * t + h].astype(jnp.float32) for h in range(2)]
                    halves.append(strip[:, t * 128 : (t + 1) * 128] * jnp.where(lane, pair[0], pair[1]))
                rows.append(jnp.concatenate(halves, 1))
            parts.append(jnp.concatenate(rows, 0))
        return parts

    numbers = [jnp.full((BLOCK, M), kept_ref[k], jnp.int32) for k in range(KEEP)]
    kept_rows = [jnp.right_shift(n, 2) for n in numbers]
    kept_cols = [jnp.bitwise_and(n, 3) for n in numbers]

    def keep_right(slot, re, im):
        right[slot, 0], right[slot, 1] = re, im

    def tiles_of(slot):
        return kept_tiles(rows.at[slot], right[slot, 0], right[slot, 1], kept_cols)

    def put(cell, tiles):
        for k, tile in enumerate(tiles):
            for row in range(8):
                send[cell * 32 + k * 8 + row] = tile[row * 8 : row * 8 + 8]

    def spread(cell):
        @pl.loop(0, 32)
        def _(step):
            z = 2 * cell + lax.div(step, 16)
            y = lax.rem(my_y + 2 + lax.rem(lax.div(step, 4), 4), SIDE)
            x = lax.rem(my_x + 2 + lax.rem(step, 4), SIDE)
            owner = (z * SIDE + y) * SIDE + x

            @pl.when(owner == me)
            def _():
                pltpu.make_async_copy(send.at[owner], recv.at[me], recv_sem).start()

            @pl.when(owner != me)
            def _():
                pltpu.make_async_remote_copy(
                    src_ref=send.at[owner], dst_ref=recv.at[me], send_sem=send_sem, recv_sem=recv_sem,
                    device_id={"energy": owner}, device_id_type=MESH,
                ).start()

    passing = pltpu.make_async_remote_copy(
        src_ref=passed, dst_ref=entered, send_sem=pass_sem.at[0], recv_sem=pass_sem.at[1],
        device_id={"chain": 1}, device_id_type=MESH,
    )

    @pl.when(chain == 0)
    def _():
        loads["b", 0].wait()
        b0, g0, b1, g1 = lefts[:4]
        b0.fill(*masked_coupling(0))
        loads["lead"].wait()
        re, im = b0.adjoint(*b0.adjoint(lead_in[0], lead_in[1]))
        loads["s", 0].wait()
        x_re, x_im = s_in[0, 0] + re, s_in[0, 1] + im
        loads["g", 0].wait()
        g0.fill(g_in[0, 0], g_in[0, 1])
        y_re, y_im = g0.adjoint(x_re, x_im)
        keep_right(0, y_re, y_im)
        state = g0.adjoint(y_re, y_im)
        loads["b", 1].wait()
        b1.fill(*masked_coupling(1))
        re, im = b1.adjoint(*b1.adjoint(*state))
        loads["s", 1].wait()
        x_re, x_im = s_in[1, 0] + re, s_in[1, 1] + im
        loads["g", 1].wait()
        g1.fill(g_in[1, 0], g_in[1, 1])
        y_re, y_im = g1.adjoint(x_re, x_im)
        keep_right(1, y_re, y_im)
        passed[0], passed[1] = g1.adjoint(y_re, y_im)
        pl.semaphore_wait(barrier, ENERGIES)
        passing.start()
        kept_left(rows.at[0], g_in[0, 0], g_in[0, 1], kept_rows)
        put(0, tiles_of(0))
        spread(0)
        kept_left(rows.at[1], g_in[1, 0], g_in[1, 1], kept_rows)
        put(1, tiles_of(1))
        spread(1)
        passing.wait_send()

    @pl.when(chain == 1)
    def _():
        g2, b3, g3, a2, c3 = lefts
        loads["s", 0].wait()
        loads["g", 0].wait()
        g2.fill(g_in[0, 0], g_in[0, 1])
        y_re, y_im = g2.adjoint(s_in[0, 0], s_in[0, 1])
        keep_right(0, y_re, y_im)
        fresh = g2.adjoint(y_re, y_im)
        kept_left(rows.at[0], g_in[0, 0], g_in[0, 1], kept_rows)
        put(0, tiles_of(0))
        loads["b", 0].wait()
        joined = g2.plain(*masked_coupling(0))
        a2.fill(*joined)
        loads["b", 1].wait()
        b3.fill(*masked_coupling(1))
        re, im = b3.adjoint(*b3.adjoint(*fresh))
        loads["s", 1].wait()
        x_re, x_im = s_in[1, 0] + re, s_in[1, 1] + im
        loads["g", 1].wait()
        g3.fill(g_in[1, 0], g_in[1, 1])
        y_re, y_im = g3.adjoint(x_re, x_im)
        keep_right(1, y_re, y_im)
        kept_left(rows.at[1], g_in[1, 0], g_in[1, 1], kept_rows)
        put(1, tiles_of(1))
        c3_re, c3_im = g3.plain(*b3.plain(*joined))
        c3.fill(c3_re, c3_im)
        kept_left(rows.at[2], *joined, kept_rows)
        kept_left(rows.at[3], c3_re, c3_im, kept_rows)
        loads["lead"].wait()
        pl.semaphore_wait(barrier, ENERGIES)
        passing.wait_recv()
        for cell, left in ((0, a2), (1, c3)):
            keep_right(cell, *left.adjoint(entered[0], entered[1]))
            tiles = kept_tiles(rows.at[2 + cell], right[cell, 0], right[cell, 1], kept_cols)
            for k in range(KEEP):
                for row in range(8):
                    at = cell * 32 + k * 8 + row
                    send[at] = send[at] + tiles[k][row * 8 : row * 8 + 8]
            spread(cell)

    everyone = recv.at[pl.ds(0, ENERGIES)]
    pltpu.make_async_copy(everyone, everyone, recv_sem).wait()

    def lag_step(step, carry):
        first, second = list(carry[:LAGS]), list(carry[LAGS:])
        window = [recv[step * 4 + i] for i in range(LAGS + 3)]
        for i in range(4):
            earlier = window[i]
            swapped = pltpu.roll(earlier, BLOCK, 1)
            for lag in range(LAGS):
                first[lag] += window[i + lag] * earlier
                second[lag] += window[i + lag] * swapped
        return (*first, *second)

    totals = lax.fori_loop(0, ENERGIES // 4, lag_step, (jnp.zeros((8, 128), jnp.float32),) * (2 * LAGS))
    for lag in range(LAGS):
        p, q = totals[lag] * (1.0 / ENERGIES), totals[LAGS + lag] * (1.0 / ENERGIES)
        sums[0, lag * 8 : lag * 8 + 8] = p + pltpu.roll(p, BLOCK, 1)
        sums[1, lag * 8 : lag * 8 + 8] = q - pltpu.roll(q, BLOCK, 1)
    even, odd = pl.ds(0, 64, stride=2), pl.ds(1, 64, stride=2)
    out_ref[even, :] = jnp.where(lane, sums[0, even, :], sums[0, odd, :])
    out_ref[odd, :] = jnp.where(lane, -sums[1, even, :], sums[1, odd, :])

    rest = send.at[pl.ds(0, ENERGIES - 1)]
    pltpu.make_async_copy(rest, rest, send_sem).wait()


def per_device(retarded, lesser_sigma, coupling, coupling_pattern, kept_blocks, lead_lesser):
    hbm = pl.BlockSpec(memory_space=pl.ANY)
    smem = pl.BlockSpec(memory_space=pltpu.SMEM)
    f32, bf16 = jnp.float32, jnp.bfloat16
    out = pl.pallas_call(
        kernel,
        out_shape=jax.ShapeDtypeStruct((LAGS * 8, 128), f32),
        in_specs=[smem, smem, hbm, hbm, hbm, hbm],
        out_specs=pl.BlockSpec(memory_space=pltpu.VMEM),
        scratch_shapes=[
            pltpu.VMEM((2, 2, M, M), f32),
            pltpu.VMEM((2, 2, M, M), f32),
            pltpu.VMEM((2, 2, M, M), f32),
            pltpu.VMEM((2, M, M), f32),
            pltpu.VMEM((5, 3, M, M), bf16),
            pltpu.VMEM((5, 3, M, M), bf16),
            pltpu.VMEM((4, KEEP, 2 * BLOCK, 2 * M), bf16),
            pltpu.VMEM((2, 2, M, M), f32),
            pltpu.VMEM((2, M, M), f32),
            pltpu.VMEM((2, M, M), f32),
            pltpu.VMEM((ENERGIES, 8, 128), f32),
            pltpu.VMEM((ENERGIES + LAGS, 8, 128), f32),
            pltpu.VMEM((2, LAGS * 8, 128), f32),
            pltpu.SemaphoreType.DMA((7,)),
            pltpu.SemaphoreType.DMA((2,)),
            pltpu.SemaphoreType.DMA,
            pltpu.SemaphoreType.DMA,
        ],
        compiler_params=pltpu.CompilerParams(collective_id=0, has_side_effects=True),
        name="green_chain",
    )(coupling_pattern, kept_blocks, retarded, lesser_sigma, coupling, lead_lesser)
    tiles = out.reshape(LAGS, 4, 2, 128)
    return jnp.transpose(tiles, (0, 2, 1, 3)).reshape(LAGS, 2, 512)


def solution(mesh):
    return jax.shard_map(
        per_device,
        mesh=mesh,
        in_specs=(
            P("energy", "chain", None, None, None),
            P("energy", "chain", None, None, None),
            P("chain", None, None, None),
            P("chain", None, None),
            P(),
            P("energy", None, None, None),
        ),
        out_specs=P(None, None, ("chain", "energy")),
        check_vma=False,
    )
```

```python
import functools

import jax
import jax.numpy as jnp
from jax import lax
from jax.experimental import pallas as pl
from jax.experimental.pallas import tpu as pltpu
from jax.sharding import PartitionSpec as P

M = 256
BLOCK = 64
NBLK = 4
KEEP = 4
LAGS = 16
ENERGIES = 64
SIDE = 4
MESH = pl.DeviceIdType.MESH
ADJ = (((1,), (1,)), ((), ()))
PLAIN = (((1,), (0,)), ((), ()))


def split(x):
    high = x.astype(jnp.bfloat16)
    return high, (x - high.astype(jnp.float32)).astype(jnp.bfloat16)


def dot3(left_h, left_l, right, dims):
    right_h, right_l = split(right)
    return lax.dot_general(
        jnp.concatenate([left_h, left_h, left_l], 1),
        jnp.concatenate([right_h, right_l, right_h], 1 if dims is ADJ else 0),
        dims,
        preferred_element_type=jnp.float32,
    )


class Left:
    def __init__(self, high, low):
        self.high, self.low = high, low

    def fill(self, re, im):
        for i, part in enumerate((re, im, re + im)):
            self.high[i], self.low[i] = split(part)

    def three(self, a, b, c, dims):
        return [dot3(self.high[i], self.low[i], x, dims) for i, x in enumerate((a, b, c))]

    def adjoint(self, re, im):
        p, q, s = self.three(re, im, re - im, ADJ)
        return p + q, s - p + q

    def plain(self, re, im):
        p, q, s = self.three(re, im, re + im, PLAIN)
        return p - q, s - p - q


def planes(ref):
    tiles = [ref[i] for i in range(16)]
    rows = [jnp.concatenate(tiles[2 * i : 2 * i + 2], 1) for i in range(8)]
    return jnp.concatenate(rows[:4], 0), jnp.concatenate(rows[4:], 0)


def put_planes(ref, re, im):
    for part, x in enumerate((re, im)):
        for r in range(NBLK):
            for t in range(2):
                ref[part * 8 + r * 2 + t] = x[r * BLOCK : (r + 1) * BLOCK, t * 128 : (t + 1) * 128]


def kernel(
    pattern_ref, kept_ref, g_hbm, s_hbm, b_hbm, lead_hbm, out_ref,
    g_in, s_in, b_in, lead_in, left_h, left_l, fresh_ref, grid0, grid1, entered, send, recv, sums,
    in_sem, pass_sem, send_sem, recv_sem,
):
    chain, me = lax.axis_index("chain"), lax.axis_index("energy")
    my_y, my_x = lax.rem(lax.div(me, SIDE), SIDE), lax.rem(me, SIDE)

    def load(i, source, target):
        return pltpu.make_async_copy(source, target, in_sem.at[i])

    loads = {}
    for cell in range(2):
        loads["b", cell] = load(cell, b_hbm.at[cell], b_in.at[cell])
        loads["s", cell] = load(2 + cell, s_hbm.at[0, cell], s_in.at[cell])
        loads["g", cell] = load(4 + cell, g_hbm.at[0, cell], g_in.at[cell])
    loads["lead"] = load(6, lead_hbm.at[0], lead_in)
    for name in (("b", 0), "lead", ("s", 0), ("g", 0), ("b", 1), ("s", 1), ("g", 1)):
        loads[name].start()

    barrier = pltpu.get_barrier_semaphore()

    for step in range(1, ENERGIES):
        other = me + step
        other = jnp.where(other >= ENERGIES, other - ENERGIES, other)
        pl.semaphore_signal(barrier, inc=1, device_id={"energy": other}, device_id_type=MESH)

    pl.semaphore_signal(barrier, inc=1, device_id={"chain": 1 - chain}, device_id_type=MESH)

    recv[pl.ds(ENERGIES, LAGS)] = jnp.zeros((LAGS, 8, 128), jnp.float32)
    lefts = [Left(left_h.at[i], left_l.at[i]) for i in range(5)]
    lane = lax.broadcasted_iota(jnp.int32, (BLOCK, 128), 1) < BLOCK

    def masked_coupling(cell):
        parts = []
        for part in range(2):
            rows = []
            for r in range(NBLK):
                strip = b_in[cell, part, r * BLOCK : (r + 1) * BLOCK, :]
                halves = []
                for t in range(NBLK // 2):
                    pair = [pattern_ref[cell, r, 2 * t + h].astype(jnp.float32) for h in range(2)]
                    halves.append(strip[:, t * 128 : (t + 1) * 128] * jnp.where(lane, pair[0], pair[1]))
                rows.append(jnp.concatenate(halves, 1))
            parts.append(jnp.concatenate(rows, 0))
        return parts

    def put(cell, ref, re, im):
        put_planes(ref, re, im)
        for k in range(KEEP):
            number = kept_ref[k]
            at = jnp.right_shift(number, 1)
            re_k, im_k = ref[at], ref[at + 8]
            odd = jnp.full((BLOCK, 128), jnp.bitwise_and(number, 1), jnp.int32) == 1
            still, moved = jnp.where(odd, im_k, re_k), pltpu.roll(jnp.where(odd, re_k, im_k), BLOCK, 1)
            tile = jnp.where(lane != odd, still, moved)
            for row in range(8):
                send[cell * 32 + k * 8 + row] = tile[row * 8 : row * 8 + 8]

    def spread(cell):
        @pl.loop(0, 32)
        def _(step):
            z = 2 * cell + lax.div(step, 16)
            y = lax.rem(my_y + 2 + lax.rem(lax.div(step, 4), 4), SIDE)
            x = lax.rem(my_x + 2 + lax.rem(step, 4), SIDE)
            owner = (z * SIDE + y) * SIDE + x

            @pl.when(owner == me)
            def _():
                pltpu.make_async_copy(send.at[owner], recv.at[me], recv_sem).start()

            @pl.when(owner != me)
            def _():
                pltpu.make_async_remote_copy(
                    src_ref=send.at[owner], dst_ref=recv.at[me], send_sem=send_sem, recv_sem=recv_sem,
                    device_id={"energy": owner}, device_id_type=MESH,
                ).start()

    passing = pltpu.make_async_remote_copy(
        src_ref=grid1, dst_ref=entered, send_sem=pass_sem.at[0], recv_sem=pass_sem.at[1],
        device_id={"chain": 1}, device_id_type=MESH,
    )

    def plus(x, y):
        return x[0] + y[0], x[1] + y[1]

    @pl.when(chain == 0)
    def _():
        loads["b", 0].wait()
        b0, g0, b1, g1 = lefts[:4]
        b0.fill(*masked_coupling(0))
        loads["lead"].wait()
        inner = b0.adjoint(*b0.adjoint(lead_in[0], lead_in[1]))
        loads["s", 0].wait()
        x = plus(inner, (s_in[0, 0], s_in[0, 1]))
        loads["g", 0].wait()
        g0.fill(g_in[0, 0], g_in[0, 1])
        state = g0.adjoint(*g0.adjoint(*x))
        put(0, grid0, *state)
        loads["b", 1].wait()
        b1.fill(*masked_coupling(1))
        inner = b1.adjoint(*b1.adjoint(*state))
        loads["s", 1].wait()
        x = plus(inner, (s_in[1, 0], s_in[1, 1]))
        loads["g", 1].wait()
        g1.fill(g_in[1, 0], g_in[1, 1])
        state = g1.adjoint(*g1.adjoint(*x))
        put(1, grid1, *state)
        pl.semaphore_wait(barrier, ENERGIES)
        passing.start()
        spread(0)
        spread(1)
        passing.wait_send()

    @pl.when(chain == 1)
    def _():
        g2, b3, g3, a2, c3 = lefts
        loads["s", 0].wait()
        loads["g", 0].wait()
        g2.fill(g_in[0, 0], g_in[0, 1])
        fresh = g2.adjoint(*g2.adjoint(s_in[0, 0], s_in[0, 1]))
        fresh_ref[0, 0], fresh_ref[0, 1] = fresh
        loads["b", 0].wait()
        joined = g2.plain(*masked_coupling(0))
        a2.fill(*joined)
        loads["b", 1].wait()
        b3.fill(*masked_coupling(1))
        inner = b3.adjoint(*b3.adjoint(*fresh))
        loads["s", 1].wait()
        x = plus(inner, (s_in[1, 0], s_in[1, 1]))
        loads["g", 1].wait()
        g3.fill(g_in[1, 0], g_in[1, 1])
        fresh_ref[1, 0], fresh_ref[1, 1] = g3.adjoint(*g3.adjoint(*x))
        c3.fill(*g3.plain(*b3.plain(*joined)))
        loads["lead"].wait()
        pl.semaphore_wait(barrier, ENERGIES)
        passing.wait_recv()
        for cell, left, ref in ((0, a2, grid0), (1, c3, grid1)):
            change = left.adjoint(*left.adjoint(*planes(entered)))
            put(cell, ref, *plus(change, (fresh_ref[cell, 0], fresh_ref[cell, 1])))
            spread(cell)

    everyone = recv.at[pl.ds(0, ENERGIES)]
    pltpu.make_async_copy(everyone, everyone, recv_sem).wait()

    def lag_step(step, carry):
        first, second = list(carry[:LAGS]), list(carry[LAGS:])
        window = [recv[step * 4 + i] for i in range(LAGS + 3)]
        for i in range(4):
            earlier = window[i]
            swapped = pltpu.roll(earlier, BLOCK, 1)
            for lag in range(LAGS):
                first[lag] += window[i + lag] * earlier
                second[lag] += window[i + lag] * swapped
        return (*first, *second)

    totals = lax.fori_loop(0, ENERGIES // 4, lag_step, (jnp.zeros((8, 128), jnp.float32),) * (2 * LAGS))
    for lag in range(LAGS):
        p, q = totals[lag], totals[LAGS + lag]
        sums[0, lag * 8 : lag * 8 + 8] = p + pltpu.roll(p, BLOCK, 1)
        sums[1, lag * 8 : lag * 8 + 8] = q - pltpu.roll(q, BLOCK, 1)
    even, odd = pl.ds(0, 64, stride=2), pl.ds(1, 64, stride=2)
    out_ref[even, :] = jnp.where(lane, sums[0, even, :], sums[0, odd, :])
    out_ref[odd, :] = jnp.where(lane, -sums[1, even, :], sums[1, odd, :])

    rest = send.at[pl.ds(0, ENERGIES - 1)]
    pltpu.make_async_copy(rest, rest, send_sem).wait()


def per_device(retarded, lesser_sigma, coupling, coupling_pattern, kept_blocks, lead_lesser):
    hbm = pl.BlockSpec(memory_space=pltpu.HBM)
    smem = pl.BlockSpec(memory_space=pltpu.SMEM)
    f32, bf16 = jnp.float32, jnp.bfloat16
    out = pl.pallas_call(
        kernel,
        out_shape=pltpu.VMEM((LAGS * 8, 128), f32),
        in_specs=[smem, smem, hbm, hbm, hbm, hbm],
        out_specs=pl.BlockSpec(memory_space=pltpu.VMEM),
        scratch_shapes=[
            pltpu.VMEM((2, 2, M, M), f32),
            pltpu.VMEM((2, 2, M, M), f32),
            pltpu.VMEM((2, 2, M, M), f32),
            pltpu.VMEM((2, M, M), f32),
            pltpu.VMEM((5, 3, M, M), bf16),
            pltpu.VMEM((5, 3, M, M), bf16),
            pltpu.VMEM((2, 2, M, M), f32),
            pltpu.VMEM((16, BLOCK, 128), f32),
            pltpu.VMEM((16, BLOCK, 128), f32),
            pltpu.VMEM((16, BLOCK, 128), f32),
            pltpu.VMEM((ENERGIES, 8, 128), f32),
            pltpu.VMEM((ENERGIES + LAGS, 8, 128), f32),
            pltpu.VMEM((2, LAGS * 8, 128), f32),
            pltpu.SemaphoreType.DMA((7,)),
            pltpu.SemaphoreType.DMA((2,)),
            pltpu.SemaphoreType.DMA,
            pltpu.SemaphoreType.DMA,
        ],
        compiler_params=pltpu.CompilerParams(collective_id=0, has_side_effects=True),
        name="green_chain",
    )(coupling_pattern, kept_blocks, retarded, lesser_sigma, coupling, lead_lesser)
    tiles = out.reshape(LAGS, 4, 2, 128)
    return jnp.transpose(tiles, (0, 2, 1, 3)).reshape(LAGS, 2, 512) * (1.0 / ENERGIES)


def solution(mesh):
    return jax.shard_map(
        per_device,
        mesh=mesh,
        in_specs=(
            P("energy", "chain", None, None, None),
            P("energy", "chain", None, None, None),
            P("chain", None, None, None),
            P("chain", None, None),
            P(),
            P("energy", None, None, None),
        ),
        out_specs=P(None, None, ("chain", "energy")),
        check_vma=False,
    )
```

```python
import functools

import jax
import jax.numpy as jnp
from jax import lax
from jax.experimental import pallas as pl
from jax.experimental.pallas import tpu as pltpu
from jax.sharding import PartitionSpec as P

M = 256
BLOCK = 64
NBLK = 4
KEEP = 4
LAGS = 16
ENERGIES = 64
SIDE = 4
MESH = pl.DeviceIdType.MESH
ADJ = (((1,), (1,)), ((), ()))
PLAIN = (((1,), (0,)), ((), ()))


def split(x):
    high = x.astype(jnp.bfloat16)
    return high, (x - high.astype(jnp.float32)).astype(jnp.bfloat16)


class Left:
    def __init__(self, high, low):
        self.high, self.low = high, low

    def fill(self, re, im):
        for i, part in enumerate((re, im, re + im)):
            self.high[i], self.low[i] = split(part)

    def times(self, parts, rows, dims):
        out = []
        for i, (right_h, right_l) in enumerate(parts):
            left_h, left_l = self.high[i, rows, :], self.low[i, rows, :]
            out.append(
                lax.dot_general(
                    jnp.concatenate([left_h, left_h, left_l], 1),
                    jnp.concatenate([right_h, right_l, right_h], 1 if dims is ADJ else 0),
                    dims,
                    preferred_element_type=jnp.float32,
                )
            )
        return out

    def adjoint(self, re, im, pieces=1):
        parts = [split(x) for x in (re, im, re - im)]
        size = M // pieces
        for piece in range(pieces):
            p, q, s = self.times(parts, slice(piece * size, (piece + 1) * size), ADJ)
            yield p + q, s - p + q

    def twice(self, re, im):
        (inner,) = self.adjoint(re, im)
        (outer,) = self.adjoint(*inner)
        return outer

    def plain(self, re, im):
        p, q, s = self.times([split(x) for x in (re, im, re + im)], slice(0, M), PLAIN)
        return p - q, s - p - q


def planes(ref):
    tiles = [ref[i] for i in range(16)]
    rows = [jnp.concatenate(tiles[2 * i : 2 * i + 2], 1) for i in range(8)]
    return jnp.concatenate(rows[:4], 0), jnp.concatenate(rows[4:], 0)


def put_planes(ref, re, im, first=0):
    for part, x in enumerate((re, im)):
        for r in range(x.shape[0] // BLOCK):
            for t in range(2):
                ref[part * 8 + (first + r) * 2 + t] = x[r * BLOCK : (r + 1) * BLOCK, t * 128 : (t + 1) * 128]


def kernel(
    pattern_hbm, kept_hbm, g_hbm, s_hbm, b_hbm, lead_hbm, out_ref,
    pattern_ref, kept_ref, g_in, s_in, b_in, lead_in, left_h, left_l, fresh_ref, joined, grid0, grid1, entered, extra, send, recv, sums,
    in_sem, pass_sem, back_sem, send_sem, recv_sem,
):
    chain, me = lax.axis_index("chain"), lax.axis_index("energy")
    my_y, my_x = lax.rem(lax.div(me, SIDE), SIDE), lax.rem(me, SIDE)

    def load(i, source, target):
        return pltpu.make_async_copy(source, target, in_sem.at[i])

    loads = {}
    for cell in range(2):
        loads["b", cell] = load(cell, b_hbm.at[cell], b_in.at[cell])
        loads["s", cell] = load(2 + cell, s_hbm.at[0, cell], s_in.at[cell])
        loads["g", cell] = load(4 + cell, g_hbm.at[0, cell], g_in.at[cell])
    loads["lead"] = load(6, lead_hbm.at[0], lead_in)
    loads["pattern"] = load(7, pattern_hbm, pattern_ref)
    loads["kept"] = load(8, kept_hbm, kept_ref)
    for name in ("pattern", ("b", 0), "lead", ("s", 0), ("g", 0), ("b", 1), ("s", 1), ("g", 1), "kept"):
        loads[name].start()

    barrier = pltpu.get_barrier_semaphore()

    for step in range(1, ENERGIES):
        other = me + step
        other = jnp.where(other >= ENERGIES, other - ENERGIES, other)
        pl.semaphore_signal(barrier, inc=1, device_id={"energy": other}, device_id_type=MESH)

    pl.semaphore_signal(barrier, inc=1, device_id={"chain": 1 - chain}, device_id_type=MESH)

    recv[pl.ds(ENERGIES, LAGS)] = jnp.zeros((LAGS, 8, 128), jnp.float32)
    lefts = [Left(left_h.at[i], left_l.at[i]) for i in range(5)]
    lane = lax.broadcasted_iota(jnp.int32, (BLOCK, 128), 1) < BLOCK

    def masked_coupling(cell):
        parts = []
        for part in range(2):
            rows = []
            for r in range(NBLK):
                strip = b_in[cell, part, r * BLOCK : (r + 1) * BLOCK, :]
                halves = []
                for t in range(NBLK // 2):
                    pair = [pattern_ref[cell, r, 2 * t + h].astype(jnp.float32) for h in range(2)]
                    halves.append(strip[:, t * 128 : (t + 1) * 128] * jnp.where(lane, pair[0], pair[1]))
                rows.append(jnp.concatenate(halves, 1))
            parts.append(jnp.concatenate(rows, 0))
        return parts

    def cut(ref):
        for k in range(KEEP):
            number = kept_ref[k]
            at = jnp.right_shift(number, 1)
            re_k, im_k = ref[at], ref[at + 8]
            odd = jnp.full((BLOCK, 128), jnp.bitwise_and(number, 1), jnp.int32) == 1
            still, moved = jnp.where(odd, im_k, re_k), pltpu.roll(jnp.where(odd, re_k, im_k), BLOCK, 1)
            tile = jnp.where(lane != odd, still, moved)
            for row in range(8):
                yield k * 8 + row, tile[row * 8 : row * 8 + 8]

    def turned(mine, by):
        at = mine + by
        return jnp.where(at >= SIDE, at - SIDE, at)

    offsets = (2, 3, 1, 0)
    across = {dx: turned(my_x, dx) for dx in offsets}
    lines = {dy: turned(my_y, dy) * SIDE for dy in offsets}

    def spread(cell):
        for dy in offsets:
            for dx in offsets:
                for z in (2 * cell, 2 * cell + 1):
                    owner = z * SIDE * SIDE + lines[dy] + across[dx]

                    def away(owner=owner):
                        pltpu.make_async_remote_copy(
                            src_ref=send.at[owner], dst_ref=recv.at[me], send_sem=send_sem, recv_sem=recv_sem,
                            device_id={"energy": owner}, device_id_type=MESH,
                        ).start()

                    def here(owner=owner):
                        pltpu.make_async_copy(send.at[owner], recv.at[me], recv_sem).start()

                    if dy or dx:
                        away()
                    else:
                        pl.when(owner != me)(away)
                        pl.when(owner == me)(here)

    def spread_next():
        for dy in offsets:
            for dx in offsets:
                for z in (0, 1):
                    owner = z * SIDE * SIDE + lines[dy] + across[dx]
                    pltpu.make_async_remote_copy(
                        src_ref=extra.at[owner], dst_ref=recv.at[me], send_sem=send_sem, recv_sem=recv_sem,
                        device_id={"chain": 1, "energy": owner}, device_id_type=MESH,
                    ).start()

    def partner_copy(source, target, sems, first, to):
        return pltpu.make_async_remote_copy(
            src_ref=source, dst_ref=target, send_sem=sems.at[first], recv_sem=sems.at[first + 1],
            device_id={"chain": to}, device_id_type=MESH,
        )

    passing = partner_copy(grid1, entered, pass_sem, 0, 1)
    back = partner_copy(joined, joined, back_sem, 0, 0)
    back_tiles = partner_copy(extra, extra, back_sem, 2, 0)

    def plus(x, y):
        return x[0] + y[0], x[1] + y[1]

    loads["pattern"].wait()

    @pl.when(chain == 0)
    def _():
        loads["b", 0].wait()
        b0, g0, b1, g1, a2 = lefts
        b0.fill(*masked_coupling(0))
        loads["lead"].wait()
        inner = b0.twice(lead_in[0], lead_in[1])
        loads["s", 0].wait()
        x = plus(inner, (s_in[0, 0], s_in[0, 1]))
        loads["g", 0].wait()
        g0.fill(g_in[0, 0], g_in[0, 1])
        state = g0.twice(*x)
        put_planes(grid0, *state)
        loads["kept"].wait()
        for at, tile in cut(grid0):
            send[at] = tile
        loads["b", 1].wait()
        b1.fill(*masked_coupling(1))
        inner = b1.twice(*state)
        loads["s", 1].wait()
        x = plus(inner, (s_in[1, 0], s_in[1, 1]))
        pl.semaphore_wait(barrier, ENERGIES)
        spread(0)
        loads["g", 1].wait()
        g1.fill(g_in[1, 0], g_in[1, 1])
        (y,) = g1.adjoint(*x)
        for half, (re, im) in enumerate(g1.adjoint(*y, pieces=2)):
            put_planes(grid1, re, im, first=2 * half)
            for part in range(2):
                piece = pl.ds(part * 8 + half * 4, 4)
                partner_copy(grid1.at[piece], entered.at[piece], pass_sem, 0, 1).start()
        back.wait_recv()
        a2.fill(joined[0], joined[1])
        put_planes(grid0, *a2.twice(*planes(grid1)))
        back_tiles.wait_recv()
        for at, tile in cut(grid0):
            extra[at] = extra[at] + tile
        spread_next()
        for at, tile in cut(grid1):
            send[32 + at] = tile
        spread(1)
        passing.wait_send()

    @pl.when(chain == 1)
    def _():
        g2, b3, g3, c3 = lefts[:4]
        loads["b", 0].wait()
        loads["g", 0].wait()
        g2.fill(g_in[0, 0], g_in[0, 1])
        joined[0], joined[1] = g2.plain(*masked_coupling(0))
        loads["s", 0].wait()
        fresh = g2.twice(s_in[0, 0], s_in[0, 1])
        put_planes(grid0, *fresh)
        loads["kept"].wait()
        for at, tile in cut(grid0):
            extra[at] = tile
        pl.semaphore_wait(barrier, ENERGIES)
        back.start()
        back_tiles.start()
        loads["b", 1].wait()
        b3.fill(*masked_coupling(1))
        inner = b3.twice(*fresh)
        loads["s", 1].wait()
        x = plus(inner, (s_in[1, 0], s_in[1, 1]))
        loads["g", 1].wait()
        g3.fill(g_in[1, 0], g_in[1, 1])
        fresh_ref[0], fresh_ref[1] = g3.twice(*x)
        c3.fill(*g3.plain(*b3.plain(joined[0], joined[1])))
        loads["lead"].wait()
        passing.wait_recv()
        put_planes(grid1, *plus(c3.twice(*planes(entered)), (fresh_ref[0], fresh_ref[1])))
        for at, tile in cut(grid1):
            send[32 + at] = tile
        spread(1)
        back.wait_send()
        back_tiles.wait_send()

    everyone = recv.at[pl.ds(0, ENERGIES)]
    pltpu.make_async_copy(everyone, everyone, recv_sem).wait()

    def lag_step(step, carry):
        first, second = list(carry[:LAGS]), list(carry[LAGS:])
        window = [recv[step * 4 + i] for i in range(LAGS + 3)]
        for i in range(4):
            earlier = window[i]
            swapped = pltpu.roll(earlier, BLOCK, 1)
            for lag in range(LAGS):
                first[lag] += window[i + lag] * earlier
                second[lag] += window[i + lag] * swapped
        return (*first, *second)

    totals = lax.fori_loop(0, ENERGIES // 4, lag_step, (jnp.zeros((8, 128), jnp.float32),) * (2 * LAGS))
    for lag in range(LAGS):
        p, q = totals[lag], totals[LAGS + lag]
        sums[0, lag * 8 : lag * 8 + 8] = p + pltpu.roll(p, BLOCK, 1)
        sums[1, lag * 8 : lag * 8 + 8] = q - pltpu.roll(q, BLOCK, 1)
    even, odd = pl.ds(0, 64, stride=2), pl.ds(1, 64, stride=2)
    out_ref[even, :] = jnp.where(lane, sums[0, even, :], sums[0, odd, :])
    out_ref[odd, :] = jnp.where(lane, -sums[1, even, :], sums[1, odd, :])

    def sent(tiles):
        some = recv.at[pl.ds(0, tiles)]
        pltpu.make_async_copy(some, some, send_sem).wait()

    @pl.when(chain == 0)
    def _():
        sent(63)
        sent(32)

    @pl.when(chain == 1)
    def _():
        sent(31)

        @pl.when(me < 32)
        def _():
            sent(1)


def per_device(retarded, lesser_sigma, coupling, coupling_pattern, kept_blocks, lead_lesser):
    hbm = pl.BlockSpec(memory_space=pltpu.HBM)
    f32, bf16 = jnp.float32, jnp.bfloat16
    out = pl.pallas_call(
        kernel,
        out_shape=pltpu.VMEM((LAGS * 8, 128), f32),
        in_specs=[hbm, hbm, hbm, hbm, hbm, hbm],
        out_specs=pl.BlockSpec(memory_space=pltpu.VMEM),
        scratch_shapes=[
            pltpu.SMEM((2, NBLK, NBLK), jnp.int32),
            pltpu.SMEM((KEEP,), jnp.int32),
            pltpu.VMEM((2, 2, M, M), f32),
            pltpu.VMEM((2, 2, M, M), f32),
            pltpu.VMEM((2, 2, M, M), f32),
            pltpu.VMEM((2, M, M), f32),
            pltpu.VMEM((5, 3, M, M), bf16),
            pltpu.VMEM((5, 3, M, M), bf16),
            pltpu.VMEM((2, M, M), f32),
            pltpu.VMEM((2, M, M), f32),
            pltpu.VMEM((16, BLOCK, 128), f32),
            pltpu.VMEM((16, BLOCK, 128), f32),
            pltpu.VMEM((16, BLOCK, 128), f32),
            pltpu.VMEM((32, 8, 128), f32),
            pltpu.VMEM((ENERGIES, 8, 128), f32),
            pltpu.VMEM((ENERGIES + LAGS, 8, 128), f32),
            pltpu.VMEM((2, LAGS * 8, 128), f32),
            pltpu.SemaphoreType.DMA((9,)),
            pltpu.SemaphoreType.DMA((2,)),
            pltpu.SemaphoreType.DMA((4,)),
            pltpu.SemaphoreType.DMA,
            pltpu.SemaphoreType.DMA,
        ],
        compiler_params=pltpu.CompilerParams(collective_id=0, has_side_effects=True),
        name="green_chain",
    )(coupling_pattern, kept_blocks, retarded, lesser_sigma, coupling, lead_lesser)
    tiles = out.reshape(LAGS, 4, 2, 128)
    return jnp.transpose(tiles, (0, 2, 1, 3)).reshape(LAGS, 2, 512) * (1.0 / ENERGIES)


def solution(mesh):
    return jax.shard_map(
        per_device,
        mesh=mesh,
        in_specs=(
            P("energy", "chain", None, None, None),
            P("energy", "chain", None, None, None),
            P("chain", None, None, None),
            P("chain", None, None),
            P(),
            P("energy", None, None, None),
        ),
        out_specs=P(None, None, ("chain", "energy")),
        check_vma=False,
    )
```

```python
import functools

import jax
import jax.numpy as jnp
from jax import lax
from jax.experimental import pallas as pl
from jax.experimental.pallas import tpu as pltpu
from jax.sharding import PartitionSpec as P

M = 256
BLOCK = 64
NBLK = 4
KEEP = 4
LAGS = 16
ENERGIES = 64
SIDE = 4
LINES = ENERGIES // SIDE
MESH = pl.DeviceIdType.MESH
ADJ = (((1,), (1,)), ((), ()))
PLAIN = (((1,), (0,)), ((), ()))


def split(x):
    high = x.astype(jnp.bfloat16)
    return high, (x - high.astype(jnp.float32)).astype(jnp.bfloat16)


class Left:
    def __init__(self, high, low):
        self.high, self.low = high, low

    def fill(self, re, im):
        for i, part in enumerate((re, im, re + im)):
            self.high[i], self.low[i] = split(part)

    def times(self, parts, rows, dims):
        out = []
        for i, (right_h, right_l) in enumerate(parts):
            left_h, left_l = self.high[i, rows, :], self.low[i, rows, :]
            out.append(
                lax.dot_general(
                    jnp.concatenate([left_h, left_h, left_l], 1),
                    jnp.concatenate([right_h, right_l, right_h], 1 if dims is ADJ else 0),
                    dims,
                    preferred_element_type=jnp.float32,
                )
            )
        return out

    def adjoint(self, re, im, pieces=1):
        parts = [split(x) for x in (re, im, re - im)]
        size = M // pieces
        for piece in range(pieces):
            p, q, s = self.times(parts, slice(piece * size, (piece + 1) * size), ADJ)
            yield p + q, s - p + q

    def twice(self, re, im):
        (inner,) = self.adjoint(re, im)
        (outer,) = self.adjoint(*inner)
        return outer

    def plain(self, re, im, pieces=1):
        parts = [split(x) for x in (re, im, re + im)]
        size = M // pieces
        for piece in range(pieces):
            p, q, s = self.times(parts, slice(piece * size, (piece + 1) * size), PLAIN)
            yield p - q, s - p - q


def put_planes(ref, re, im, first=0):
    for part, x in enumerate((re, im)):
        for r in range(x.shape[0] // BLOCK):
            for t in range(2):
                ref[part * 8 + (first + r) * 2 + t] = x[r * BLOCK : (r + 1) * BLOCK, t * 128 : (t + 1) * 128]


def kernel(
    pattern_hbm, kept_hbm, g_hbm, s_hbm, b_hbm, lead_hbm, out_ref,
    pattern_ref, kept_ref, g_in, s_in, b_in, lead_in, left_h, left_l, fresh_ref, joined, grid0, grid1, leaving, entered, g_far, extra, send, recv, seen, seen_swapped, sums,
    in_sem, pass_sem, back_sem, send_sem, recv_sem, hello, go,
):
    chain, me = lax.axis_index("chain"), lax.axis_index("energy")
    my_y, my_x = lax.rem(lax.div(me, SIDE), SIDE), lax.rem(me, SIDE)

    def load(i, source, target):
        return pltpu.make_async_copy(source, target, in_sem.at[i])

    loads = {}
    for cell in range(2):
        loads["b", cell] = load(cell, b_hbm.at[cell], b_in.at[cell])
        loads["s", cell] = load(2 + cell, s_hbm.at[0, cell], s_in.at[cell])
        loads["g", cell] = load(4 + cell, g_hbm.at[0, cell], g_in.at[cell])
    loads["lead"] = load(6, lead_hbm.at[0], lead_in)
    loads["pattern"] = load(7, pattern_hbm, pattern_ref)
    loads["kept"] = load(8, kept_hbm, kept_ref)
    for name in ("pattern", ("b", 0), "lead", ("g", 0), ("s", 0), ("g", 1), ("b", 1), ("s", 1), "kept"):
        loads[name].start()

    barrier = pltpu.get_barrier_semaphore()

    def turned(mine, by):
        at = mine + by
        return jnp.where(at >= SIDE, at - SIDE, at)

    my_z = lax.div(me, SIDE * SIDE)
    offsets = (2, 3, 1, 0)
    across = {dx: turned(my_x, dx) for dx in offsets}
    lines = {dy: turned(my_y, dy) * SIDE for dy in offsets}
    planes_of = {dz: turned(my_z, dz) * SIDE * SIDE for dz in offsets}
    steps = [(dz, dy, dx) for dz in offsets for dy in offsets for dx in offsets]
    furthest_first = sorted(steps, key=lambda step: -sum(min(d, SIDE - d) for d in step))

    @pl.when(chain == 1)
    def _():
        pl.semaphore_signal(barrier, inc=1, device_id={"chain": 0}, device_id_type=MESH)

    for ref in (seen, seen_swapped):
        ref[...] = jnp.zeros_like(ref)

    def announce():
        for dz, dy, dx in furthest_first[:-1]:
            other = planes_of[dz] + lines[dy] + across[dx]
            pl.semaphore_signal(barrier, inc=1, device_id={"chain": 1, "energy": other}, device_id_type=MESH)

    my_line = lax.div(me, SIDE)
    arrived = recv_sem.at[my_line]
    lefts = [Left(left_h.at[i], left_l.at[i]) for i in range(5)]
    lane = lax.broadcasted_iota(jnp.int32, (BLOCK, 128), 1) < BLOCK

    def masked_coupling(cell):
        parts = []
        for part in range(2):
            rows = []
            for r in range(NBLK):
                strip = b_in[cell, part, r * BLOCK : (r + 1) * BLOCK, :]
                halves = []
                for t in range(NBLK // 2):
                    pair = [pattern_ref[cell, r, 2 * t + h].astype(jnp.float32) for h in range(2)]
                    halves.append(strip[:, t * 128 : (t + 1) * 128] * jnp.where(lane, pair[0], pair[1]))
                rows.append(jnp.concatenate(halves, 1))
            parts.append(jnp.concatenate(rows, 0))
        return parts

    def cut(ref):
        for k in range(KEEP):
            number = kept_ref[k]
            at = jnp.right_shift(number, 1)
            re_k, im_k = ref[at], ref[at + 8]
            odd = jnp.full((BLOCK, 128), jnp.bitwise_and(number, 1), jnp.int32) == 1
            still, moved = jnp.where(odd, im_k, re_k), pltpu.roll(jnp.where(odd, re_k, im_k), BLOCK, 1)
            tile = jnp.where(lane != odd, still, moved)
            for row in range(8):
                yield k * 8 + row, tile[row * 8 : row * 8 + 8]

    def spread(cell):
        for dy in offsets:
            for dx in offsets:
                for z in (2 * cell, 2 * cell + 1):
                    owner = z * SIDE * SIDE + lines[dy] + across[dx]

                    def away(owner=owner):
                        pltpu.make_async_remote_copy(
                            src_ref=send.at[owner], dst_ref=recv.at[me], send_sem=send_sem, recv_sem=arrived,
                            device_id={"energy": owner}, device_id_type=MESH,
                        ).start()

                    def here(owner=owner):
                        pltpu.make_async_copy(send.at[owner], recv.at[me], arrived).start()

                    if dy or dx:
                        away()
                    else:
                        pl.when(owner != me)(away)
                        pl.when(owner == me)(here)

    def spread_next():
        for dy in offsets:
            for dx in offsets:
                for z in (0, 1):
                    owner = z * SIDE * SIDE + lines[dy] + across[dx]
                    pltpu.make_async_remote_copy(
                        src_ref=extra.at[owner], dst_ref=recv.at[me], send_sem=send_sem, recv_sem=arrived,
                        device_id={"chain": 1, "energy": owner}, device_id_type=MESH,
                    ).start()

    def partner_copy(source, target, sems, first, to):
        return pltpu.make_async_remote_copy(
            src_ref=source, dst_ref=target, send_sem=sems.at[first], recv_sem=sems.at[first + 1],
            device_id={"chain": to}, device_id_type=MESH,
        )


    def plus(x, y):
        return x[0] + y[0], x[1] + y[1]

    loads["pattern"].wait()

    passing = partner_copy(leaving, entered, pass_sem, 0, 1)
    passing_g = partner_copy(g_hbm.at[0, 1], g_far, pass_sem, 2, 1)
    back = partner_copy(joined, joined, back_sem, 0, 0)
    back_tiles = partner_copy(extra, extra, back_sem, 2, 0)

    @pl.when(chain == 0)
    def _():
        pl.semaphore_signal(barrier, inc=1, device_id={"chain": 1}, device_id_type=MESH)
        pl.semaphore_wait(barrier, 1)
        passing_g.start()
        pl.semaphore_signal(hello, inc=1, device_id={"chain": 1}, device_id_type=MESH)

    announce()

    def wait_for(*names):
        for name in names:
            loads[name].wait()

    @pl.when(chain == 0)
    def _():
        b0, g0, b1, g1, d2 = lefts
        wait_for(("b", 0))
        b0.fill(*masked_coupling(0))
        wait_for("lead", ("s", 0), ("g", 0))
        (inner,) = b0.adjoint(lead_in[0], lead_in[1])
        g0.fill(g_in[0, 0], g_in[0, 1])
        (inner,) = b0.adjoint(*inner)
        (y,) = g0.adjoint(*plus(inner, (s_in[0, 0], s_in[0, 1])))
        wait_for(("b", 1), ("s", 1), ("g", 1), "kept")
        b1.fill(*masked_coupling(1))
        (state,) = g0.adjoint(*y)
        put_planes(grid0, *state)
        (inner,) = b1.adjoint(*state)
        for at, tile in cut(grid0):
            send[at] = tile
        for half, pair in enumerate(b1.adjoint(*inner, pieces=2)):
            some = pl.ds(half * (M // 2), M // 2)
            for part in range(2):
                leaving[part, some, :] = pair[part] + s_in[1, part, some, :]
                partner_copy(leaving.at[part, some], entered.at[part, some], pass_sem, 0, 1).start()
        back.wait_recv()
        d2.fill(joined[0], joined[1])
        put_planes(grid1, *d2.twice(leaving[0], leaving[1]))
        back_tiles.wait_recv()
        for at, tile in cut(grid1):
            extra[at] = extra[at] + tile
        pl.semaphore_wait(go, 1)
        spread_next()
        spread(0)
        g1.fill(g_in[1, 0], g_in[1, 1])
        put_planes(grid0, *g1.twice(leaving[0], leaving[1]))
        for at, tile in cut(grid0):
            send[32 + at] = tile
        spread(1)
        passing.wait_send()
        passing_g.wait_send()

    @pl.when(chain == 1)
    def _():
        g2, b3, g3, a2, d3 = lefts
        wait_for(("g", 0))
        g2.fill(g_in[0, 0], g_in[0, 1])
        wait_for(("b", 0), ("s", 0))
        a2.fill(*next(g2.plain(*masked_coupling(0))))
        fresh = g2.twice(s_in[0, 0], s_in[0, 1])
        wait_for(("b", 1), ("g", 1), ("s", 1), "kept", "lead")
        passing_g.wait_recv()
        pl.semaphore_wait(hello, 1)
        for half, pair in enumerate(a2.plain(g_far[0], g_far[1], pieces=2)):
            some = pl.ds(half * (M // 2), M // 2)
            for part in range(2):
                joined[part, some, :] = pair[part]
                partner_copy(joined.at[part, some], joined.at[part, some], back_sem, 0, 0).start()
        put_planes(grid0, *fresh)
        for at, tile in cut(grid0):
            extra[at] = tile
        back_tiles.start()
        b3.fill(*masked_coupling(1))
        (inner,) = b3.adjoint(*fresh)
        g3.fill(g_in[1, 0], g_in[1, 1])
        (inner,) = b3.adjoint(*inner)
        (bridge,) = b3.plain(joined[0], joined[1])
        (inner,) = g3.adjoint(*plus(inner, (s_in[1, 0], s_in[1, 1])))
        pl.semaphore_wait(barrier, 2 * ENERGIES - 1)
        pl.semaphore_signal(go, inc=1, device_id={"chain": 0}, device_id_type=MESH)
        (state,) = g3.adjoint(*inner)
        fresh_ref[0], fresh_ref[1] = state
        d3.fill(*next(g3.plain(*bridge)))
        passing.wait_recv()
        put_planes(grid1, *plus(d3.twice(entered[0], entered[1]), (fresh_ref[0], fresh_ref[1])))
        for at, tile in cut(grid1):
            send[32 + at] = tile
        spread(1)
        back.wait_send()
        back_tiles.wait_send()

    order = (0, 1, 3, 2)

    def line_step(step, carry):
        first, second = list(carry[:LAGS]), list(carry[LAGS:])
        z = turned(my_z, order[step // SIDE])
        y = turned(my_y, order[step % SIDE])
        line = z * SIDE + y
        mine = recv.at[pl.ds(line * SIDE, SIDE)]
        pltpu.make_async_copy(mine, mine, recv_sem.at[line]).wait()
        base = line * SIDE + LAGS
        new = [recv[line * SIDE + i] for i in range(SIDE)]
        swapped = [pltpu.roll(tile, BLOCK, 1) for tile in new]
        for i in range(SIDE):
            seen[base + i] = new[i]
            seen_swapped[base + i] = swapped[i]
        for ahead in range(LAGS + SIDE - 1):
            later = new[ahead] if ahead < SIDE else seen[base + ahead]
            for i in range(SIDE):
                lag = ahead - i
                if 0 <= lag < LAGS:
                    first[lag] += later * new[i]
                    second[lag] += later * swapped[i]
        for behind in range(1, LAGS):
            earlier, earlier_swapped = seen[base - behind], seen_swapped[base - behind]
            for i in range(SIDE):
                lag = behind + i
                if lag < LAGS:
                    first[lag] += new[i] * earlier
                    second[lag] += new[i] * earlier_swapped
        return (*first, *second)

    totals = (jnp.zeros((8, 128), jnp.float32),) * (2 * LAGS)
    for step in range(LINES):
        totals = line_step(step, totals)
    for lag in range(LAGS):
        p, q = totals[lag], totals[LAGS + lag]
        sums[0, lag * 8 : lag * 8 + 8] = p + pltpu.roll(p, BLOCK, 1)
        sums[1, lag * 8 : lag * 8 + 8] = q - pltpu.roll(q, BLOCK, 1)
    even, odd = pl.ds(0, 64, stride=2), pl.ds(1, 64, stride=2)
    out_ref[even, :] = jnp.where(lane, sums[0, even, :], sums[0, odd, :])
    out_ref[odd, :] = jnp.where(lane, -sums[1, even, :], sums[1, odd, :])

    def sent(tiles):
        some = recv.at[pl.ds(0, tiles)]
        pltpu.make_async_copy(some, some, send_sem).wait()

    @pl.when(chain == 0)
    def _():
        sent(63)
        sent(32)

    @pl.when(chain == 1)
    def _():
        sent(31)

        @pl.when(me < 32)
        def _():
            sent(1)


def per_device(retarded, lesser_sigma, coupling, coupling_pattern, kept_blocks, lead_lesser):
    hbm = pl.BlockSpec(memory_space=pltpu.HBM)
    f32, bf16 = jnp.float32, jnp.bfloat16
    out = pl.pallas_call(
        kernel,
        out_shape=pltpu.VMEM((LAGS * 8, 128), f32),
        in_specs=[hbm, hbm, hbm, hbm, hbm, hbm],
        out_specs=pl.BlockSpec(memory_space=pltpu.VMEM),
        scratch_shapes=[
            pltpu.SMEM((2, NBLK, NBLK), jnp.int32),
            pltpu.SMEM((KEEP,), jnp.int32),
            pltpu.VMEM((2, 2, M, M), f32),
            pltpu.VMEM((2, 2, M, M), f32),
            pltpu.VMEM((2, 2, M, M), f32),
            pltpu.VMEM((2, M, M), f32),
            pltpu.VMEM((5, 3, M, M), bf16),
            pltpu.VMEM((5, 3, M, M), bf16),
            pltpu.VMEM((2, M, M), f32),
            pltpu.VMEM((2, M, M), f32),
            pltpu.VMEM((16, BLOCK, 128), f32),
            pltpu.VMEM((16, BLOCK, 128), f32),
            pltpu.VMEM((2, M, M), f32),
            pltpu.VMEM((2, M, M), f32),
            pltpu.VMEM((2, M, M), f32),
            pltpu.VMEM((32, 8, 128), f32),
            pltpu.VMEM((ENERGIES, 8, 128), f32),
            pltpu.VMEM((ENERGIES, 8, 128), f32),
            pltpu.VMEM((ENERGIES + 2 * LAGS, 8, 128), f32),
            pltpu.VMEM((ENERGIES + 2 * LAGS, 8, 128), f32),
            pltpu.VMEM((2, LAGS * 8, 128), f32),
            pltpu.SemaphoreType.DMA((9,)),
            pltpu.SemaphoreType.DMA((4,)),
            pltpu.SemaphoreType.DMA((4,)),
            pltpu.SemaphoreType.DMA,
            pltpu.SemaphoreType.DMA((LINES,)),
            pltpu.SemaphoreType.REGULAR,
            pltpu.SemaphoreType.REGULAR,
        ],
        compiler_params=pltpu.CompilerParams(collective_id=0, has_side_effects=True),
        name="green_chain",
    )(coupling_pattern, kept_blocks, retarded, lesser_sigma, coupling, lead_lesser)
    tiles = out.reshape(LAGS, 4, 2, 128)
    return jnp.transpose(tiles, (0, 2, 1, 3)).reshape(LAGS, 2, 512) * (1.0 / ENERGIES)


def solution(mesh):
    return jax.shard_map(
        per_device,
        mesh=mesh,
        in_specs=(
            P("energy", "chain", None, None, None),
            P("energy", "chain", None, None, None),
            P("chain", None, None, None),
            P("chain", None, None),
            P(),
            P("energy", None, None, None),
        ),
        out_specs=P(None, None, ("chain", "energy")),
        check_vma=False,
    )
```

```python
import functools

import jax
import jax.numpy as jnp
from jax import lax
from jax.experimental import pallas as pl
from jax.experimental.pallas import tpu as pltpu
from jax.sharding import PartitionSpec as P

M = 256
BLOCK = 64
NBLK = 4
KEEP = 4
LAGS = 16
ENERGIES = 64
SIDE = 4
LINES = ENERGIES // SIDE
MESH = pl.DeviceIdType.MESH
ADJ = (((1,), (1,)), ((), ()))
PLAIN = (((1,), (0,)), ((), ()))


def split(x):
    high = x.astype(jnp.bfloat16)
    return high, (x - high.astype(jnp.float32)).astype(jnp.bfloat16)


class Left:
    def __init__(self, high, low):
        self.high, self.low = high, low

    def fill(self, re, im):
        for i, part in enumerate((re, im, re + im)):
            self.high[i], self.low[i] = split(part)

    def times(self, parts, rows, dims):
        out = []
        for i, (right_h, right_l) in enumerate(parts):
            left_h, left_l = self.high[i, rows, :], self.low[i, rows, :]
            out.append(
                lax.dot_general(
                    jnp.concatenate([left_h, left_h, left_l], 1),
                    jnp.concatenate([right_h, right_l, right_h], 1 if dims is ADJ else 0),
                    dims,
                    preferred_element_type=jnp.float32,
                )
            )
        return out

    def adjoint(self, re, im, pieces=1):
        parts = [split(x) for x in (re, im, re - im)]
        size = M // pieces
        for piece in range(pieces):
            p, q, s = self.times(parts, slice(piece * size, (piece + 1) * size), ADJ)
            yield p + q, s - p + q

    def twice(self, re, im):
        (inner,) = self.adjoint(re, im)
        (outer,) = self.adjoint(*inner)
        return outer

    def plain(self, re, im, pieces=1):
        parts = [split(x) for x in (re, im, re + im)]
        size = M // pieces
        for piece in range(pieces):
            p, q, s = self.times(parts, slice(piece * size, (piece + 1) * size), PLAIN)
            yield p - q, s - p - q


def put_planes(ref, re, im, first=0):
    for part, x in enumerate((re, im)):
        for r in range(x.shape[0] // BLOCK):
            for t in range(2):
                ref[part * 8 + (first + r) * 2 + t] = x[r * BLOCK : (r + 1) * BLOCK, t * 128 : (t + 1) * 128]


def kernel(
    pattern_hbm, kept_hbm, g_hbm, s_hbm, b_hbm, lead_hbm, out_ref,
    pattern_ref, kept_ref, g_in, s_in, b_in, lead_in, left_h, left_l, fresh_ref, joined, grid0, grid1, leaving, entered, g_far, extra, send, recv, seen, seen_swapped, sums,
    in_sem, pass_sem, back_sem, send_sem, recv_sem, hello, go,
):
    chain, me = lax.axis_index("chain"), lax.axis_index("energy")
    my_y, my_x = lax.rem(lax.div(me, SIDE), SIDE), lax.rem(me, SIDE)

    def load(i, source, target):
        return pltpu.make_async_copy(source, target, in_sem.at[i])

    loads = {}
    for cell in range(2):
        loads["b", cell] = load(cell, b_hbm.at[cell], b_in.at[cell])
        loads["s", cell] = load(2 + cell, s_hbm.at[0, cell], s_in.at[cell])
        loads["g", cell] = load(4 + cell, g_hbm.at[0, cell], g_in.at[cell])
    loads["lead"] = load(6, lead_hbm.at[0], lead_in)
    loads["pattern"] = load(7, pattern_hbm, pattern_ref)
    loads["kept"] = load(8, kept_hbm, kept_ref)
    for name in ("pattern", ("b", 0), "lead", ("g", 0), ("s", 0), ("g", 1), ("b", 1), ("s", 1), "kept"):
        loads[name].start()

    barrier = pltpu.get_barrier_semaphore()

    def turned(mine, by):
        at = mine + by
        return jnp.where(at >= SIDE, at - SIDE, at)

    my_z = lax.div(me, SIDE * SIDE)
    offsets = (2, 3, 1, 0)
    across = {dx: turned(my_x, dx) for dx in offsets}
    lines = {dy: turned(my_y, dy) * SIDE for dy in offsets}
    planes_of = {dz: turned(my_z, dz) * SIDE * SIDE for dz in offsets}
    steps = [(dz, dy, dx) for dz in offsets for dy in offsets for dx in offsets]
    furthest_first = sorted(steps, key=lambda step: -sum(min(d, SIDE - d) for d in step))

    @pl.when(chain == 1)
    def _():
        pl.semaphore_signal(barrier, inc=1, device_id={"chain": 0}, device_id_type=MESH)

    for ref in (seen, seen_swapped):
        ref[...] = jnp.zeros_like(ref)

    def announce():
        for dz, dy, dx in furthest_first[:-1]:
            other = planes_of[dz] + lines[dy] + across[dx]
            pl.semaphore_signal(barrier, inc=1, device_id={"chain": 1, "energy": other}, device_id_type=MESH)

    my_line = lax.div(me, SIDE)
    arrived = recv_sem.at[my_line]
    lefts = [Left(left_h.at[i], left_l.at[i]) for i in range(5)]
    lane = lax.broadcasted_iota(jnp.int32, (BLOCK, 128), 1) < BLOCK

    def masked_coupling(cell):
        parts = []
        for part in range(2):
            rows = []
            for r in range(NBLK):
                strip = b_in[cell, part, r * BLOCK : (r + 1) * BLOCK, :]
                halves = []
                for t in range(NBLK // 2):
                    pair = [pattern_ref[cell, r, 2 * t + h].astype(jnp.float32) for h in range(2)]
                    halves.append(strip[:, t * 128 : (t + 1) * 128] * jnp.where(lane, pair[0], pair[1]))
                rows.append(jnp.concatenate(halves, 1))
            parts.append(jnp.concatenate(rows, 0))
        return parts

    def cut(ref):
        for k in range(KEEP):
            number = kept_ref[k]
            at = jnp.right_shift(number, 1)
            re_k, im_k = ref[at], ref[at + 8]
            odd = jnp.full((BLOCK, 128), jnp.bitwise_and(number, 1), jnp.int32) == 1
            still, moved = jnp.where(odd, im_k, re_k), pltpu.roll(jnp.where(odd, re_k, im_k), BLOCK, 1)
            tile = jnp.where(lane != odd, still, moved)
            for row in range(8):
                yield k * 8 + row, tile[row * 8 : row * 8 + 8]

    def spread(cell):
        for dy in offsets:
            for dx in offsets:
                for z in (2 * cell, 2 * cell + 1):
                    owner = z * SIDE * SIDE + lines[dy] + across[dx]

                    def away(owner=owner):
                        pltpu.make_async_remote_copy(
                            src_ref=send.at[owner], dst_ref=recv.at[me], send_sem=send_sem, recv_sem=arrived,
                            device_id={"energy": owner}, device_id_type=MESH,
                        ).start()

                    def here(owner=owner):
                        pltpu.make_async_copy(send.at[owner], recv.at[me], arrived).start()

                    if dy or dx:
                        away()
                    else:
                        pl.when(owner != me)(away)
                        pl.when(owner == me)(here)

    def spread_next():
        for dy in offsets:
            for dx in offsets:
                for z in (0, 1):
                    owner = z * SIDE * SIDE + lines[dy] + across[dx]
                    pltpu.make_async_remote_copy(
                        src_ref=extra.at[owner], dst_ref=recv.at[me], send_sem=send_sem, recv_sem=arrived,
                        device_id={"chain": 1, "energy": owner}, device_id_type=MESH,
                    ).start()

    def partner_copy(source, target, sems, first, to):
        return pltpu.make_async_remote_copy(
            src_ref=source, dst_ref=target, send_sem=sems.at[first], recv_sem=sems.at[first + 1],
            device_id={"chain": to}, device_id_type=MESH,
        )


    def plus(x, y):
        return x[0] + y[0], x[1] + y[1]

    loads["pattern"].wait()

    passing = partner_copy(leaving, entered, pass_sem, 0, 1)
    passing_g = partner_copy(g_hbm.at[0, 1], g_far, pass_sem, 2, 1)
    back = partner_copy(joined, joined, back_sem, 0, 0)
    back_tiles = partner_copy(extra, extra, back_sem, 2, 0)

    @pl.when(chain == 0)
    def _():
        pl.semaphore_signal(barrier, inc=1, device_id={"chain": 1}, device_id_type=MESH)
        pl.semaphore_wait(barrier, 1)
        passing_g.start()
        pl.semaphore_signal(hello, inc=1, device_id={"chain": 1}, device_id_type=MESH)

    announce()

    def wait_for(*names):
        for name in names:
            loads[name].wait()

    @pl.when(chain == 0)
    def _():
        b0, g0, b1, g1, d2 = lefts
        wait_for(("b", 0))
        b0.fill(*masked_coupling(0))
        wait_for("lead", ("s", 0), ("g", 0))
        (inner,) = b0.adjoint(lead_in[0], lead_in[1])
        g0.fill(g_in[0, 0], g_in[0, 1])
        (inner,) = b0.adjoint(*inner)
        (y,) = g0.adjoint(*plus(inner, (s_in[0, 0], s_in[0, 1])))
        wait_for(("b", 1), ("s", 1), ("g", 1), "kept")
        b1.fill(*masked_coupling(1))
        (state,) = g0.adjoint(*y)
        put_planes(grid0, *state)
        (inner,) = b1.adjoint(*state)
        for at, tile in cut(grid0):
            send[at] = tile
        for half, pair in enumerate(b1.adjoint(*inner, pieces=2)):
            some = pl.ds(half * (M // 2), M // 2)
            for part in range(2):
                leaving[part, some, :] = pair[part] + s_in[1, part, some, :]
                partner_copy(leaving.at[part, some], entered.at[part, some], pass_sem, 0, 1).start()
        back.wait_recv()
        d2.fill(joined[0], joined[1])
        put_planes(grid1, *d2.twice(leaving[0], leaving[1]))
        back_tiles.wait_recv()
        for at, tile in cut(grid1):
            extra[at] = extra[at] + tile
        pl.semaphore_wait(go, 1)
        spread_next()
        spread(0)
        g1.fill(g_in[1, 0], g_in[1, 1])
        put_planes(grid0, *g1.twice(leaving[0], leaving[1]))
        for at, tile in cut(grid0):
            send[32 + at] = tile
        spread(1)
        passing.wait_send()
        passing_g.wait_send()

    @pl.when(chain == 1)
    def _():
        g2, b3, g3, a2, d3 = lefts
        wait_for(("g", 0))
        g2.fill(g_in[0, 0], g_in[0, 1])
        wait_for(("b", 0), ("s", 0))
        a2.fill(*next(g2.plain(*masked_coupling(0))))
        (inner,) = g2.adjoint(s_in[0, 0], s_in[0, 1])
        wait_for(("b", 1), ("g", 1), ("s", 1), "kept", "lead")
        passing_g.wait_recv()
        pl.semaphore_wait(hello, 1)
        for half, pair in enumerate(a2.plain(g_far[0], g_far[1], pieces=2)):
            some = pl.ds(half * (M // 2), M // 2)
            for part in range(2):
                joined[part, some, :] = pair[part]
                partner_copy(joined.at[part, some], joined.at[part, some], back_sem, 0, 0).start()
        (fresh,) = g2.adjoint(*inner)
        put_planes(grid0, *fresh)
        for at, tile in cut(grid0):
            extra[at] = tile
        back_tiles.start()
        b3.fill(*masked_coupling(1))
        (inner,) = b3.adjoint(*fresh)
        g3.fill(g_in[1, 0], g_in[1, 1])
        (inner,) = b3.adjoint(*inner)
        (bridge,) = b3.plain(joined[0], joined[1])
        (inner,) = g3.adjoint(*plus(inner, (s_in[1, 0], s_in[1, 1])))
        pl.semaphore_wait(barrier, 2 * ENERGIES - 1)
        pl.semaphore_signal(go, inc=1, device_id={"chain": 0}, device_id_type=MESH)
        (state,) = g3.adjoint(*inner)
        fresh_ref[0], fresh_ref[1] = state
        d3.fill(*next(g3.plain(*bridge)))
        passing.wait_recv()
        put_planes(grid1, *plus(d3.twice(entered[0], entered[1]), (fresh_ref[0], fresh_ref[1])))
        for at, tile in cut(grid1):
            send[32 + at] = tile
        spread(1)
        back.wait_send()
        back_tiles.wait_send()

    order = (0, 1, 3, 2)

    def line_step(step, carry):
        first, second = list(carry[:LAGS]), list(carry[LAGS:])
        z = turned(my_z, order[step // SIDE])
        y = turned(my_y, order[step % SIDE])
        line = z * SIDE + y
        mine = recv.at[pl.ds(line * SIDE, SIDE)]
        pltpu.make_async_copy(mine, mine, recv_sem.at[line]).wait()
        base = line * SIDE + LAGS
        new = [recv[line * SIDE + i] for i in range(SIDE)]
        swapped = [pltpu.roll(tile, BLOCK, 1) for tile in new]
        for i in range(SIDE):
            seen[base + i] = new[i]
            seen_swapped[base + i] = swapped[i]
        for ahead in range(LAGS + SIDE - 1):
            later = new[ahead] if ahead < SIDE else seen[base + ahead]
            for i in range(SIDE):
                lag = ahead - i
                if 0 <= lag < LAGS:
                    first[lag] += later * new[i]
                    second[lag] += later * swapped[i]
        for behind in range(1, LAGS):
            earlier, earlier_swapped = seen[base - behind], seen_swapped[base - behind]
            for i in range(SIDE):
                lag = behind + i
                if lag < LAGS:
                    first[lag] += new[i] * earlier
                    second[lag] += new[i] * earlier_swapped
        return (*first, *second)

    totals = (jnp.zeros((8, 128), jnp.float32),) * (2 * LAGS)
    for step in range(LINES):
        totals = line_step(step, totals)
    for lag in range(LAGS):
        p, q = totals[lag], totals[LAGS + lag]
        sums[0, lag * 8 : lag * 8 + 8] = p + pltpu.roll(p, BLOCK, 1)
        sums[1, lag * 8 : lag * 8 + 8] = q - pltpu.roll(q, BLOCK, 1)
    even, odd = pl.ds(0, 64, stride=2), pl.ds(1, 64, stride=2)
    out_ref[even, :] = jnp.where(lane, sums[0, even, :], sums[0, odd, :])
    out_ref[odd, :] = jnp.where(lane, -sums[1, even, :], sums[1, odd, :])

    def sent(tiles):
        some = recv.at[pl.ds(0, tiles)]
        pltpu.make_async_copy(some, some, send_sem).wait()

    @pl.when(chain == 0)
    def _():
        sent(63)
        sent(32)

    @pl.when(chain == 1)
    def _():
        sent(31)

        @pl.when(me < 32)
        def _():
            sent(1)


def per_device(retarded, lesser_sigma, coupling, coupling_pattern, kept_blocks, lead_lesser):
    hbm = pl.BlockSpec(memory_space=pltpu.HBM)
    f32, bf16 = jnp.float32, jnp.bfloat16
    out = pl.pallas_call(
        kernel,
        out_shape=pltpu.VMEM((LAGS * 8, 128), f32),
        in_specs=[hbm, hbm, hbm, hbm, hbm, hbm],
        out_specs=pl.BlockSpec(memory_space=pltpu.VMEM),
        scratch_shapes=[
            pltpu.SMEM((2, NBLK, NBLK), jnp.int32),
            pltpu.SMEM((KEEP,), jnp.int32),
            pltpu.VMEM((2, 2, M, M), f32),
            pltpu.VMEM((2, 2, M, M), f32),
            pltpu.VMEM((2, 2, M, M), f32),
            pltpu.VMEM((2, M, M), f32),
            pltpu.VMEM((5, 3, M, M), bf16),
            pltpu.VMEM((5, 3, M, M), bf16),
            pltpu.VMEM((2, M, M), f32),
            pltpu.VMEM((2, M, M), f32),
            pltpu.VMEM((16, BLOCK, 128), f32),
            pltpu.VMEM((16, BLOCK, 128), f32),
            pltpu.VMEM((2, M, M), f32),
            pltpu.VMEM((2, M, M), f32),
            pltpu.VMEM((2, M, M), f32),
            pltpu.VMEM((32, 8, 128), f32),
            pltpu.VMEM((ENERGIES, 8, 128), f32),
            pltpu.VMEM((ENERGIES, 8, 128), f32),
            pltpu.VMEM((ENERGIES + 2 * LAGS, 8, 128), f32),
            pltpu.VMEM((ENERGIES + 2 * LAGS, 8, 128), f32),
            pltpu.VMEM((2, LAGS * 8, 128), f32),
            pltpu.SemaphoreType.DMA((9,)),
            pltpu.SemaphoreType.DMA((4,)),
            pltpu.SemaphoreType.DMA((4,)),
            pltpu.SemaphoreType.DMA,
            pltpu.SemaphoreType.DMA((LINES,)),
            pltpu.SemaphoreType.REGULAR,
            pltpu.SemaphoreType.REGULAR,
        ],
        compiler_params=pltpu.CompilerParams(collective_id=0, has_side_effects=True),
        name="green_chain",
    )(coupling_pattern, kept_blocks, retarded, lesser_sigma, coupling, lead_lesser)
    tiles = out.reshape(LAGS, 4, 2, 128)
    return jnp.transpose(tiles, (0, 2, 1, 3)).reshape(LAGS, 2, 512) * (1.0 / ENERGIES)


def solution(mesh):
    return jax.shard_map(
        per_device,
        mesh=mesh,
        in_specs=(
            P("energy", "chain", None, None, None),
            P("energy", "chain", None, None, None),
            P("chain", None, None, None),
            P("chain", None, None),
            P(),
            P("energy", None, None, None),
        ),
        out_specs=P(None, None, ("chain", "energy")),
        check_vma=False,
    )
```
